1024 devices in a mesh: pipe: 16 (over z), tensor: 16 (over y, x_lo), dp: 4 (over x_hi, core).
Axes of the slice: x: 4 (x_hi: 2, x_lo: 2; x = x_hi * 2 + x_lo), y: 8, z: 16, core: 2. Of those that a mesh axis runs over, the one named last changes fastest.
Arguments:
- entry_grads: float32 [2, 16, 128, 3584], P(None, 'pipe', ('dp', 'tensor')), may hold values from -6 to 6
- fresh_grads: float32 [2, 2, 128, 3584], P(None, None, ('dp', 'tensor')), may hold values from -6 to 6
- saved_inputs: bfloat16 [2, 3, 16, 128, 3584], P(None, None, 'pipe', 'dp'), may hold values from -6 to 6
- w_in: bfloat16 [2, 16, 3584, 2048], P(None, 'pipe', None, 'tensor'), may hold values from -0.09375 to 0.09375
- w_down: bfloat16 [2, 16, 1024, 3584], P(None, 'pipe', 'tensor'), may hold values from -0.1875 to 0.1875
Outputs:
- hand_offs: float32 [2, 3, 16, 128, 3584], P(None, None, 'pipe', ('dp', 'tensor'))
- grad_w_in: float32 [2, 16, 3584, 2048], P(None, 'pipe', 'dp', 'tensor')
- grad_w_down: float32 [2, 16, 1024, 3584], P(None, 'pipe', 'tensor', 'dp')
The draws below stay inside these ranges and needn't reach their ends.
All inputs are finite; a program needn't handle non-finite values.
Results may differ from the reference program's by a relative error of at most 0.02.
Values may be sent and summed in bfloat16 or wider, within the bound.
A program may use at most 64 MiB of HBM per device.

```python
import jax
import jax.numpy as jnp
from jax import lax

D = 3584
HID = 1024
K_STEPS = 3
MB_ROWS = 32
SECTIONS = 16
ROWS = 128
HSH = 64
N_TENSOR = 16
N_DP = 4


def level_of(own_key, extent, shards, smallest, top_value):
    def one(dim, blocks):
        draws = jax.random.uniform(jax.random.fold_in(jax.random.fold_in(own_key, 6), dim), (blocks,), jnp.float32, smallest / len(shards), top_value / len(shards))
        return jnp.repeat(jnp.exp(draws), extent[dim] // blocks).reshape((-1,) + (1,) * (len(extent) - dim - 1))

    level = one(*shards[0])
    for cut in shards[1:]:
        level = level * one(*cut)
    return level


def normal_values(key, shape, scale, limit, pieces=(), held_as=jnp.bfloat16):
    result = jax.random.normal(key, shape, jnp.float32) * scale
    if len(pieces) > 0:
        result = level_of(key, shape, pieces, -0.22, 0.18) * result
    return jnp.clip(result, min=-limit, max=limit).astype(held_as)


def setup_inputs(seed: int = 0) -> dict:
    keys = jax.random.split(jax.random.key(seed), 6)
    entry_grads = normal_values(keys[0], (2, SECTIONS, ROWS, D), 1.0, 6.0, ((1, 16), (2, 64)), jnp.float32)
    fresh_grads = normal_values(keys[1], (2, K_STEPS - 1, ROWS, D), 1.0, 6.0, ((2, 64),), jnp.float32)
    saved_inputs = normal_values(keys[2], (2, K_STEPS, SECTIONS, ROWS, D), 1.0, 6.0, ((2, 16), (3, 4)))
    w_in = normal_values(keys[3], (2, SECTIONS, D, 2 * HID), D ** -0.5, 0.09375, ((1, 16), (3, 16)))
    w_down = normal_values(keys[4], (2, SECTIONS, HID, D), HID ** -0.5, 0.1875, ((1, 16), (2, 16)))
    return {"entry_grads": entry_grads, "fresh_grads": fresh_grads, "saved_inputs": saved_inputs, "w_in": w_in, "w_down": w_down}


def block_grads(inputs, incoming, w_in_layer, w_down_layer):
    projected = jnp.dot(inputs, w_in_layer, preferred_element_type=jnp.float32)
    projected = projected.reshape(ROWS, N_TENSOR, 2, HSH)
    gate_part = projected[:, :, 0, :].reshape(ROWS, HID)
    up_part = projected[:, :, 1, :].reshape(ROWS, HID)
    sigmoid_val = jax.nn.sigmoid(gate_part)
    activated = gate_part * sigmoid_val
    hidden = (activated * up_part).astype(jnp.bfloat16)
    dy_rows = incoming.astype(jnp.bfloat16)
    hidden_grad = jnp.dot(dy_rows, w_down_layer.T, preferred_element_type=jnp.float32)
    gate_grad = hidden_grad * up_part * sigmoid_val * (1.0 + gate_part * (1.0 - sigmoid_val))
    up_grad = hidden_grad * activated
    pre_grad = jnp.stack([gate_grad.reshape(ROWS, N_TENSOR, HSH), up_grad.reshape(ROWS, N_TENSOR, HSH)], axis=2)
    pre_grad = pre_grad.reshape(ROWS, 2 * HID).astype(jnp.bfloat16)
    parts = jnp.einsum('rtc,dtc->trd', pre_grad.reshape(ROWS, N_TENSOR, 2 * HSH).astype(jnp.float32),
                       w_in_layer.reshape(D, N_TENSOR, 2 * HSH).astype(jnp.float32))
    rounded = lax.optimization_barrier(parts.astype(jnp.bfloat16)).astype(jnp.float32)
    handed = incoming + jnp.sum(rounded, axis=0)
    in_term = jnp.einsum('nrd,nrc->ndc', inputs.reshape(N_DP, MB_ROWS, D).astype(jnp.float32),
                         pre_grad.reshape(N_DP, MB_ROWS, 2 * HID).astype(jnp.float32))
    down_term = jnp.einsum('nrh,nrd->nhd', hidden.reshape(N_DP, MB_ROWS, HID).astype(jnp.float32),
                           dy_rows.reshape(N_DP, MB_ROWS, D).astype(jnp.float32))
    return handed, in_term, down_term


def replica_total(terms):
    rounded = lax.optimization_barrier(terms.astype(jnp.bfloat16)).astype(jnp.float32)
    return jnp.sum(rounded, axis=0)


def reference(entry_grads, fresh_grads, saved_inputs, w_in, w_down):
    results = {}
    in_grads = {}
    down_grads = {}
    for direction in range(2):
        if direction == 0:
            order = list(range(SECTIONS - 1, -1, -1))
        else:
            order = list(range(SECTIONS))
        for section in order:
            in_accum = jnp.zeros((N_DP, D, 2 * HID), jnp.float32)
            down_accum = jnp.zeros((N_DP, HID, D), jnp.float32)
            for window_step in range(K_STEPS):
                if window_step == 0:
                    incoming = entry_grads[direction, section]
                else:
                    neighbour = section + 1 if direction == 0 else section - 1
                    if 0 <= neighbour < SECTIONS:
                        incoming = results[(direction, window_step - 1, neighbour)]
                    else:
                        incoming = fresh_grads[direction, window_step - 1]
                handed, in_term, down_term = block_grads(saved_inputs[direction, window_step, section], incoming,
                                                         w_in[direction, section], w_down[direction, section])
                results[(direction, window_step, section)] = handed
                in_accum = in_accum + in_term
                down_accum = down_accum + down_term
            in_grads[(direction, section)] = replica_total(in_accum)
            down_grads[(direction, section)] = replica_total(down_accum)
    hand_offs = jnp.stack([jnp.stack([jnp.stack([results[(direction, window_step, section)] for section in range(SECTIONS)])
                                      for window_step in range(K_STEPS)]) for direction in range(2)])
    grad_w_in = jnp.stack([jnp.stack([in_grads[(direction, section)] for section in range(SECTIONS)]) for direction in range(2)])
    grad_w_down = jnp.stack([jnp.stack([down_grads[(direction, section)] for section in range(SECTIONS)]) for direction in range(2)])
    return hand_offs, grad_w_in, grad_w_down
```

```python
import jax
import jax.numpy as jnp
from jax import lax
from jax.experimental import pallas as pl
from jax.experimental.pallas import tpu as pltpu
from jax.sharding import PartitionSpec as P

MESH = pl.DeviceIdType.MESH
ORDER = (4, 3, 5, 2, 6, 1, 7, 0)
FAR = (4, 3, 5, 2, 6, 1, 7)
NT = (((1,), (1,)), ((), ()))
TN = (((0,), (0,)), ((), ()))


def relay(
    entry,
    fresh,
    xin,
    w_in,
    w_down,
    hand,
    gwi,
    gwd,
    wcat,
    wdd,
    xv,
    ste,
    stf,
    gent,
    dyg,
    ps,
    dhs,
    dhx,
    abx,
    wp,
    rs,
    nb,
    hs,
    xg,
    pgg,
    hb,
    dyx,
    ab,
    gi,
    gd,
    lsem,
    ent_s,
    ent_r,
    fre_s,
    fre_r,
    ag_s,
    ag_r,
    ab_s,
    ab_r,
    wd_s,
    wd_r,
    we_s,
    we_r,
    px_s,
    px_r,
    wp_s,
    wp_r,
    wq_s,
    wq_r,
    rs_s,
    rs_r,
    hand_s,
    hand_r,
    xg_s,
    xg_r,
    hb_s,
    hb_r,
    pg_s,
    pg_r,
    dy_s,
    dy_r,
    out_sem,
):
    f32 = jnp.float32
    bf16 = jnp.bfloat16
    steps = xv.shape[1]
    w = gent.shape[2]
    pipe = lax.axis_index("pipe")
    t = lax.axis_index("tensor")
    r = lax.axis_index("dp")
    sections = lax.axis_size("pipe")
    y = t // 2
    x = t % 2
    g = t // 4
    s = t % 4
    below = (pipe + sections - 1) % sections
    above = (pipe + 1) % sections
    across = 2 * y + 1 - x
    partner = (pipe, across, r)
    core = r % 2
    xhi = r // 2
    peers = (r, 2 * xhi + 1 - core, 2 * (1 - xhi) + core, 2 * (1 - xhi) + 1 - core)

    neighbours = (partner, (pipe, across, peers[2]))

    def rcopy(src, dst, ssem, rsem, dev):
        return pltpu.make_async_remote_copy(
            src_ref=src, dst_ref=dst, send_sem=ssem, recv_sem=rsem, device_id=dev, device_id_type=MESH
        )

    sent = []
    held = []

    def send(src, dst, ssem, rsem, dev):
        copy = rcopy(src, dst, ssem, rsem, dev)
        copy.start()
        sent.append(copy)

    def landed(ref, ssem, rsem):
        rcopy(ref, ref, ssem, rsem, partner).wait_recv()

    def cols(c):
        return pl.ds(pl.multiple_of(c * w, 128), w)

    def send_x(q, k):
        send(xin.at[:, k, 0, :, cols(peers[q])], xg.at[q, :, k], xg_s.at[k, q], xg_r.at[k, q], (pipe, t if q == 1 else across, peers[q]))

    loads = [
        pltpu.make_async_copy(w_in.at[0, 0], wcat.at[:, pl.ds(0, 128)], lsem.at[0]),
        pltpu.make_async_copy(w_in.at[1, 0], wcat.at[:, pl.ds(128, 128)], lsem.at[1]),
        pltpu.make_async_copy(xin.at[:, :, 0], xv, lsem.at[2]),
    ]
    for d in range(2):
        for i in range(2):
            loads.append(
                pltpu.make_async_copy(
                    w_down.at[d, 0, :, cols(x + 2 * i)],
                    wdd.at[pl.ds(128 * d, 64), pl.ds(i * w, w)],
                    lsem.at[3 + 2 * d + i],
                )
            )
    own_x = pltpu.make_async_copy(xin.at[:, :, 0, :, cols(r)], xg.at[0], lsem.at[7])
    own_e = pltpu.make_async_copy(entry.at[:, 0, :, cols(s)], ste.at[s], ent_r.at[s])
    own_f = pltpu.make_async_copy(fresh.at[:, :, :, cols(s)], stf.at[s], fre_r.at[s])
    own_e.start()
    for copy in loads:
        copy.start()
    own_f.start()
    own_x.start()

    barrier = pltpu.get_barrier_semaphore()
    greet = [(pipe, 2 * ((y + off) % 8) + x, r) for off in range(1, 8)]
    greet.append(partner)
    greet.append((pipe, 4 * g + (3 - s), r))
    for off in range(8):
        greet.append((below, 2 * ((y + off) % 8) + x, r))
        greet.append((above, 2 * ((y + off) % 8) + x, r))
    for q in range(1, 4):
        greet.append((pipe, t, peers[q]))
        greet.append((pipe, across, peers[q]))
    for dev in greet:
        pl.semaphore_signal(barrier, inc=1, device_id=dev, device_id_type=MESH)
    pl.semaphore_wait(barrier, len(greet))

    def half(d):
        return pl.ds(pl.multiple_of(128 * d, 128), 128)

    def down_part(i, d):
        return wdd.at[pl.ds(pl.multiple_of(128 * d + 64, 64), 64), pl.ds(i * w, w)]

    for off in range(1, 4):
        c = (s + off) % 4
        send(entry.at[:, 0, :, cols(c)], ste.at[s], ent_s.at[off], ent_r.at[s], (pipe, 4 * g + c, r))
    for i in range(2):
        send(
            w_down.at[core, 0, :, cols(1 - x + 2 * i)],
            down_part(i, core),
            wd_s.at[i],
            wd_r.at[i],
            neighbours[i],
        )
    for i in range(2):
        send(
            w_in.at[core, 0, cols(1 - x + 2 * i), :],
            wp.at[i, :, half(core)],
            wp_s.at[i],
            wp_r.at[i],
            neighbours[i],
        )
    for copy in loads[:3]:
        copy.wait()
    rows_all = xv[...].reshape(2 * steps * 32, 4 * w)
    proj = jnp.dot(rows_all, wcat[...], preferred_element_type=f32)
    lanes = lax.broadcasted_iota(jnp.int32, (64, 128), 1)
    rows = lax.broadcasted_iota(jnp.int32, (64, 128), 0)
    left = lanes < 64
    first = (rows // 8) % 2 == 0
    for k in range(steps):
        pieces = []
        for gg in range(4):
            for d in range(2):
                base = d * steps * 32 + k * 32 + 8 * gg
                pieces.append(proj[base : base + 8, 128 * d : 128 * d + 128])
        both = jnp.concatenate(pieces, axis=0)
        swapped = pltpu.roll(both, 64, 1)
        gate = jnp.where(left, both, swapped)
        up = jnp.where(left, swapped, both)
        sig = jax.nn.sigmoid(gate)
        act = gate * sig
        ab[k] = jnp.where(left, up * sig * (1.0 + gate * (1.0 - sig)), act)
        hb[0, k] = jnp.where(left == first, act * up, 0.0).astype(bf16)
    for k in range(steps):
        send(ab.at[k], abx.at[k], ab_s.at[k], ab_r.at[k], partner)
    for src in range(4):
        pltpu.make_async_copy(ste.at[src], ste.at[src], ent_r.at[src]).wait()
    for src in range(4):
        for d in range(2):
            gent[0, pl.ds(8 * d + 2 * src, 2), :] = ste[src, d]
    mine = pl.ds(pl.multiple_of(16 * g, 16), 16)
    dyg[0, y % 2, mine, :] = gent[0].astype(bf16)

    def place(k, src_y, d):
        if k == 0:
            return dyg.at[k, src_y % 2, pl.ds(pl.multiple_of(16 * (src_y // 2), 16), 16), :]
        return dyg.at[k, src_y % 2, pl.ds(pl.multiple_of(16 * (src_y // 2) + 8 * d, 8), 8), :]

    own0 = place(0, y, 0)
    for off in ORDER[:-1]:
        yy = (y + off) % 8
        send(own0, own0, ag_s.at[0, 0, off], ag_r.at[0, 0, y], (pipe, 2 * yy + x, r))
    for off in range(1, 4):
        c = (s + off) % 4
        send(fresh.at[:, :, :, cols(c)], stf.at[s], fre_s.at[off], fre_r.at[s], (pipe, 4 * g + c, r))
    for k in range(steps):
        send_x(1, k)

    for q in range(1, 4):
        send(hb.at[0], hb.at[q], hb_s.at[q], hb_r.at[q], (pipe, t, peers[q]))

    for i in range(2):
        landed(down_part(i, core), wd_s.at[i], wd_r.at[i])
        send(down_part(i, core), down_part(i, core), we_s.at[i], we_r.at[i], (pipe, t, peers[1]))
    for i in range(2):
        ref = wp.at[i, :, half(core)]
        landed(ref, wp_s.at[i], wp_r.at[i])
        send(ref, ref, wq_s.at[i], wq_r.at[i], (pipe, t, peers[1]))

    def send_dy(k):
        turn = (core + x) % 2
        send(dyg.at[k, 1 - xhi], dyx.at[2 + turn, k], dy_s.at[k, 2], dy_r.at[k, 2 + turn], (pipe, t, x + 2 * (1 - xhi)))
        send(dyg.at[k, 1 - xhi], dyx.at[2 + turn, k], dy_s.at[k, 3], dy_r.at[k, 2 + turn], (pipe, across, x + 2 * (1 - xhi)))
        send(dyg.at[k, xhi], dyx.at[turn, k], dy_s.at[k, 1], dy_r.at[k, turn], (pipe, across, x + 2 * xhi))
        stays = pltpu.make_async_copy(dyg.at[k, xhi], dyx.at[0, k], dy_r.at[k, 0])
        goes = rcopy(dyg.at[k, xhi], dyx.at[1, k], dy_s.at[k, 0], dy_r.at[k, 1], (pipe, t, peers[1]))
        pl.when(core == x)(stays.start)
        pl.when(core != x)(goes.start)
        held.append(goes)

    def in_blocks(v):
        zero = jnp.zeros_like(v)
        return jnp.concatenate([jnp.where(first, v, zero), jnp.where(first, zero, v)], axis=1).astype(bf16)

    def gather(k):
        for off in ORDER:
            yy = (y + off) % 8
            if k == 0 and off == 0:
                continue
            for d in range(1) if k == 0 else range(2):
                landed(place(k, yy, d), ag_s.at[k, d, off], ag_r.at[k, d, yy])

    def grads_in(k):
        for q in range(1, 4):
            landed(xg.at[q, :, k], xg_s.at[k, q], xg_r.at[k, q])
            landed(pgg.at[q, k], pg_s.at[k, q], pg_r.at[k, q])
        if k == 0:
            own_x.wait()
        for d in range(2):
            lhs = xg[:, d, k].reshape(128, w)
            rhs = pgg[:, k, d].reshape(128, 128)
            term = lax.dot_general(lhs, rhs, TN, preferred_element_type=f32)
            gi[d] = term if k == 0 else gi[d] + term

    def grads_down(k):
        for q in range(4):
            if k == 0 and q > 0:
                landed(hb.at[q], hb_s.at[q], hb_r.at[q])
            pltpu.make_async_copy(dyx.at[q, k], dyx.at[q, k], dy_r.at[k, q]).wait()
        lhs = hb[:, k].reshape(256, 128)
        rhs = dyx[:, k].reshape(256, w)
        term = lax.dot_general(lhs, rhs, TN, preferred_element_type=f32)
        gd[...] = term if k == 0 else gd[...] + term

    outs = []

    def leave(src, dst, n):
        copy = pltpu.make_async_copy(src, dst, out_sem.at[n])
        copy.start()
        outs.append(copy)

    for k in range(steps):
        gather(k)
        if k == 0:
            for copy in loads[3:]:
                copy.wait()
            for i in range(2):
                landed(down_part(i, 1 - core), we_s.at[i], we_r.at[i])
        acc = jnp.zeros((64, 256), f32)
        for i in range(2):
            acc += lax.dot_general(dyg[k, i], wdd[:, i * w : (i + 1) * w], NT, preferred_element_type=f32)
        partial = jnp.where(first, acc[:, :128], acc[:, 128:])
        dhs[k] = partial.astype(bf16)
        send(dhs.at[k], dhx.at[k], px_s.at[k], px_r.at[k], partner)
        if k + 1 == steps:
            send_dy(k)
        landed(abx.at[k], ab_s.at[k], ab_r.at[k])
        if k == 0:
            for i in range(2):
                landed(wp.at[i, :, half(1 - core)], wq_s.at[i], wq_r.at[i])
        landed(dhx.at[k], px_s.at[k], px_r.at[k])
        dh = partial + pltpu.roll(dhx[k].astype(f32), 64, 1)
        turned = pltpu.roll(dh, 64, 1)
        pg = jnp.where(left, dh, turned) * ab[k]
        blocks = in_blocks(pg)
        other = in_blocks(jnp.where(left, turned, dh) * abx[k])
        order = (y % 2, 1 - y % 2)
        for n, offs in enumerate(((4, 2, 6, 0), (3, 5, 1, 7))):
            i = order[n]
            part = lax.dot_general(blocks, wcat[cols(x + 2 * i), :], NT, preferred_element_type=f32)
            part += lax.dot_general(other, wp[i], NT, preferred_element_type=f32)
            ps[k, i] = part.astype(bf16)
            for off in offs:
                yy = (y + off) % 8
                src = ps.at[k, i, pl.ds(pl.multiple_of(16 * (yy // 2), 16), 16), :]
                if off != 0:
                    send(src, rs.at[k, y], rs_s.at[k, off], rs_r.at[k, y], (pipe, 2 * yy + x, r))
        rs[k, y] = ps[k, y % 2, mine, :]
        for d in range(2):
            picked = jnp.concatenate([pg[16 * gg + 8 * d : 16 * gg + 8 * d + 8] for gg in range(4)], axis=0)
            pgg[0, k, d] = picked.astype(bf16)
        for q in range(1, 4):
            send(pgg.at[0, k], pgg.at[q, k], pg_s.at[k, q], pg_r.at[k, q], (pipe, t, peers[q]))
        if k + 1 < steps:
            send_dy(k)
        for m in {0: (0, 1), 1: (2,)}.get(k, ()):
            for q in range(2, 4):
                send_x(q, m)
        if k >= 1:
            grads_in(k - 1)
            grads_down(k - 1)
        if k == 0:
            for src in range(4):
                pltpu.make_async_copy(stf.at[src], stf.at[src], fre_r.at[src]).wait()
            for m in range(1, steps):
                for src in range(4):
                    for d in range(2):
                        gent[m, pl.ds(8 * d + 2 * src, 2), :] = stf[src, d, m - 1]
        for off in FAR:
            yy = (y + off) % 8
            landed(rs.at[k, yy], rs_s.at[k, off], rs_r.at[k, yy])
        total = gent[0] if k == 0 else dyg[k, y % 2, mine, :].astype(f32)
        for src in range(8):
            total += rs[k, src].astype(f32)
        if k + 1 < steps:
            upper = lax.broadcasted_iota(jnp.int32, (16, w), 0) < 8
            use_fresh = jnp.logical_or(
                jnp.logical_and(upper, pipe == 0), jnp.logical_and(jnp.logical_not(upper), pipe == sections - 1)
            )
            nb[k] = jnp.where(use_fresh, gent[k + 1], total).astype(bf16)
            for off in ORDER:
                yy = (y + off) % 8
                for d, dest in ((0, below), (1, above)):
                    send(
                        nb.at[k, pl.ds(8 * d, 8), :],
                        place(k + 1, y, d),
                        ag_s.at[k + 1, d, off],
                        ag_r.at[k + 1, d, y],
                        (dest, 2 * yy + x, r),
                    )
        for dst in range(4):
            for d in range(2):
                hs[k, dst, d] = total[8 * d + 2 * dst : 8 * d + 2 * dst + 2, :]
        for off in range(1, 4):
            dst = (s + off) % 4
            send(
                hs.at[k, dst],
                hand.at[:, k, 0, :, cols(s)],
                hand_s.at[k, off],
                hand_r.at[k, s],
                (pipe, 4 * g + dst, r),
            )
        pltpu.make_async_copy(hs.at[k, s], hand.at[:, k, 0, :, cols(s)], hand_r.at[k, s]).start()
    grads_in(steps - 1)
    for d in range(2):
        leave(gi.at[d], gwi.at[d, 0], d)
    grads_down(steps - 1)
    for d in range(2):
        leave(gd.at[pl.ds(64 * d, 64), :], gwd.at[d, 0], 2 + d)
    for k in range(steps):
        for src in range(4):
            ref = hand.at[:, k, 0, :, pl.ds(src * w, w)]
            pltpu.make_async_copy(ref, ref, hand_r.at[k, src]).wait()
    for copy in sent:
        copy.wait_send()
    for copy in held:
        pl.when(core != x)(copy.wait_send)
    for copy in outs:
        copy.wait()


def hand_out(a, b, c, a_out, b_out, c_out, sems):
    copies = [pltpu.make_async_copy(src, dst, sems.at[n]) for n, (src, dst) in enumerate(((b, b_out), (c, c_out), (a, a_out)))]
    for copy in copies:
        copy.start()
    for copy in copies:
        copy.wait()


def local(entry_grads, fresh_grads, saved_inputs, w_in, w_down):
    f32 = jnp.float32
    bf16 = jnp.bfloat16
    steps = saved_inputs.shape[1]
    width = saved_inputs.shape[4]
    w = width // 4
    vm = pltpu.VMEM
    dma = pltpu.SemaphoreType.DMA
    scratch = [
        vm((width, 256), bf16),
        vm((256, 2 * w), bf16),
        vm((2, steps, 32, width), bf16),
        vm((4, 2, 2, w), f32),
        vm((4, 2, 2, 2, w), f32),
        vm((steps, 16, w), f32),
        vm((steps, 2, 64, w), bf16),
        vm((steps, 2, 64, w), bf16),
        vm((steps, 64, 128), bf16),
        vm((steps, 64, 128), bf16),
        vm((steps, 64, 128), f32),
        vm((2, w, 256), bf16),
        vm((steps, 8, 16, w), bf16),
        vm((steps - 1, 16, w), bf16),
        vm((steps, 4, 2, 2, w), f32),
        vm((4, 2, steps, 32, w), bf16),
        vm((4, steps, 2, 32, 128), bf16),
        vm((4, steps, 64, 128), bf16),
        vm((4, steps, 64, w), bf16),
        vm((steps, 64, 128), f32),
        vm((2, w, 128), f32),
        vm((128, w), f32),
        dma((8,)),
        dma((4,)),
        dma((4,)),
        dma((4,)),
        dma((4,)),
        dma((steps, 2, 8)),
        dma((steps, 2, 8)),
        dma((steps,)),
        dma((steps,)),
        dma((2,)),
        dma((2,)),
        dma((2,)),
        dma((2,)),
        dma((steps,)),
        dma((steps,)),
        dma((2,)),
        dma((2,)),
        dma((2,)),
        dma((2,)),
        dma((steps, 8)),
        dma((steps, 8)),
        dma((steps, 4)),
        dma((steps, 4)),
        dma((steps, 4)),
        dma((steps, 4)),
        dma((4,)),
        dma((4,)),
        dma((steps, 4)),
        dma((steps, 4)),
        dma((steps, 4)),
        dma((steps, 4)),
        dma((4,)),
    ]
    anyspec = pl.BlockSpec(memory_space=pl.ANY)
    results = pl.pallas_call(
        relay,
        out_shape=(
            jax.ShapeDtypeStruct((2, steps, 1, 2, width), f32),
            jax.ShapeDtypeStruct((2, 1, w, 128), f32),
            jax.ShapeDtypeStruct((2, 1, 64, w), f32),
        ),
        in_specs=[pl.BlockSpec(memory_space=pltpu.HBM)] * 5,
        out_specs=(anyspec,) * 3,
        scratch_shapes=scratch,
        compiler_params=pltpu.CompilerParams(
            collective_id=0, has_side_effects=True, vmem_limit_bytes=52 * 1024 * 1024
        ),
    )(
        pltpu.with_memory_space_constraint(entry_grads, pltpu.HBM),
        pltpu.with_memory_space_constraint(fresh_grads, pltpu.HBM),
        saved_inputs,
        w_in,
        w_down,
    )
    return pl.pallas_call(
        hand_out,
        out_shape=tuple(jax.ShapeDtypeStruct(v.shape, v.dtype) for v in results),
        in_specs=[anyspec] * 3,
        out_specs=(pl.BlockSpec(memory_space=pltpu.HBM),) * 3,
        scratch_shapes=[dma((3,))],
        compiler_params=pltpu.CompilerParams(vmem_limit_bytes=4 * 1024 * 1024),
    )(*results)


def solution(mesh):
    placed = (
        P(None, "pipe", ("dp", "tensor"), None),
        P(None, None, ("dp", "tensor"), None),
        P(None, None, "pipe", "dp", None),
        P(None, "pipe", None, "tensor"),
        P(None, "pipe", "tensor", None),
    )
    return jax.shard_map(
        local,
        mesh=mesh,
        in_specs=placed,
        out_specs=(
            P(None, None, "pipe", ("dp", "tensor"), None),
            P(None, "pipe", "dp", "tensor"),
            P(None, "pipe", "tensor", "dp"),
        ),
        check_vma=False,
    )
```
